256 devices in a mesh: gx: 4 (over x), gy: 8 (over y, core), gz: 8 (over z).
Axes of the slice: x: 4, y: 4, z: 8, core: 2. Of those that a mesh axis runs over, the one named last changes fastest.
Arguments:
- fields: float32 [3, 64, 128, 1024], P(None, 'gx', 'gy', 'gz'), may hold values from -6 to 6
- diffusivity: float32 [64, 128, 1024], P('gx', 'gy', 'gz'), may hold values from 0.03 to 0.15
- velocity: float32 [3, 64, 128, 1024], P(None, 'gx', 'gy', 'gz'), may hold values from -2.4 to 2.4
- stored_snapshots: bfloat16 [127, 786432], P(None, ('gx', 'gy', 'gz')), may hold values from -36 to 36
- sample_index: int32 [262144], P(('gx', 'gy', 'gz')), may hold values from 0 to 32767, as said below
Outputs:
- new_fields: float32 [3, 64, 128, 1024], P(None, 'gx', 'gy', 'gz')
- snapshot_r: float32 [128, 128], replicated
The draws below stay inside these ranges and needn't reach their ends.
Inputs may be any that keep to these rules, and one draw needn't show every extreme that they name: `sample_index`: entry k of a tile's list lies between k * 32 and (k + 1) * 32 - 1.
All inputs are finite; a program needn't handle non-finite values.
Results may differ from the reference program's by a relative error of at most 0.0003.
Values sent between devices are 32-bit elements; how exact they have to be, the bound alone decides.
A program may use at most 64 MiB of HBM per device.

```python
import math
import jax
import jax.numpy as jnp
from jax import lax

CX = 16
CY = 16
CZ = 128
STRIDE = 32
SNAPS = 128
TILES = 256
SAMPLES = 1024
ROWS_DEV = 3072
ROWS = 786432
NX = 64
NY = 128
NZ = 1024
N_GX = 4
N_GY = 8
N_GZ = 8


def draw_stored_snapshots(key, part):
    key_noise, key_cols, key_rows = jax.random.split(key, 3)
    shape = (SNAPS - 1, TILES, ROWS_DEV)
    noise = jnp.clip(jax.random.normal(key_noise, shape, jnp.float32), -5.0, 5.0)
    col_scale = jnp.exp(jax.random.uniform(key_cols, (SNAPS - 1, TILES, 1), jnp.float32, math.log(0.3), math.log(3.0)))
    row_scale = jnp.exp(jax.random.uniform(key_rows, (1, TILES, ROWS_DEV), jnp.float32, math.log(0.5), math.log(2.0)))
    values = noise * col_scale * row_scale
    return values.reshape(SNAPS - 1, TILES * ROWS_DEV).astype(jnp.bfloat16)


def draw_sample_index(key, part):
    offsets = jax.random.randint(key, (TILES, SAMPLES), 0, STRIDE, jnp.int32)
    offsets = offsets.at[:, 0].set(0)
    offsets = offsets.at[:, SAMPLES - 1].set(STRIDE - 1)
    starts = jnp.arange(SAMPLES, dtype=jnp.int32) * STRIDE
    return (starts[None, :] + offsets).reshape(TILES * SAMPLES).astype(jnp.int32)


def block_levels(own_key, shape, cuts, smallest, largest):
    def one(dim, blocks):
        steps = jax.random.uniform(jax.random.fold_in(jax.random.fold_in(own_key, 6), dim), (blocks,), jnp.float32, smallest / len(cuts), largest / len(cuts))
        return jnp.repeat(jnp.exp(steps), shape[dim] // blocks).reshape((-1,) + (1,) * (len(shape) - dim - 1))

    loudness = one(*cuts[0])
    for cut in cuts[1:]:
        loudness = loudness * one(*cut)
    return loudness


def bell_draw(key, shape, deviation, most, cuts=(), kind=jnp.bfloat16):
    values = jax.random.normal(key, shape, jnp.float32) * deviation
    if len(cuts) > 0:
        values = block_levels(key, shape, cuts, -0.22, 0.18) * values
    return jnp.clip(values, min=-most, max=most).astype(kind)


def setup_inputs(seed: int = 0) -> dict:
    splits = jax.random.split(jax.random.key(seed), 6)
    fields = bell_draw(splits[0], (3, NX, NY, NZ), 1.0, 6.0, ((1, 4), (2, 8), (3, 8)), jnp.float32)
    diffusivity = jnp.clip(jnp.exp(math.log(0.15) - 1.609438 * jax.random.uniform(splits[1], (NX, NY, NZ), jnp.float32) ** block_levels(splits[1], (NX, NY, NZ), ((0, 4), (1, 8), (2, 8)), -0.2, 0.2)), 0.03, 0.15)
    velocity = bell_draw(splits[2], (3, NX, NY, NZ), 0.4, 2.4, ((1, 4), (2, 8), (3, 8)), jnp.float32)
    stored_snapshots = draw_stored_snapshots(jax.random.fold_in(splits[5], 71), 0)
    sample_index = draw_sample_index(jax.random.fold_in(splits[5], 71), 0)
    return {"fields": fields, "diffusivity": diffusivity, "velocity": velocity, "stored_snapshots": stored_snapshots, "sample_index": sample_index}


def face_term(center_u, center_k, center_v, plus_u, plus_k, plus_v, minus_u, minus_k, minus_v):
    return 0.5 * (plus_k + center_k) * (plus_u - center_u) - 0.5 * (center_k + minus_k) * (center_u - minus_u) - 0.5 * (plus_v * plus_u - minus_v * minus_u)

def reference(fields, diffusivity, velocity, stored_snapshots, sample_index):
    padded_u = jnp.pad(fields, ((0, 0), (1, 1), (1, 1), (1, 1)))
    padded_k = jnp.pad(diffusivity, ((1, 1), (1, 1), (1, 1)))
    padded_v = jnp.pad(velocity, ((0, 0), (1, 1), (1, 1), (1, 1)))
    inner = (slice(1, -1), slice(1, -1), slice(1, -1))
    terms = []
    for dim in range(3):
        upper = list(inner)
        lower = list(inner)
        upper[dim] = slice(2, None)
        lower[dim] = slice(None, -2)
        upper = tuple(upper)
        lower = tuple(lower)
        terms.append(face_term(fields, diffusivity, velocity[dim], padded_u[(slice(None),) + upper], padded_k[upper], padded_v[dim][upper], padded_u[(slice(None),) + lower], padded_k[lower], padded_v[dim][lower]))
    new_fields = fields + (terms[0] + terms[1] + terms[2])
    tiles = new_fields.reshape(3, N_GX, CX, N_GY, CY, N_GZ, CZ).transpose(1, 3, 5, 0, 2, 4, 6)
    tiles = tiles.reshape(TILES, 3, CX * CY * CZ)
    index = sample_index.reshape(TILES, SAMPLES).astype(jnp.int32)
    sampled = jnp.take_along_axis(tiles, index[:, None, :], axis=2).reshape(TILES, ROWS_DEV).astype(jnp.bfloat16)

    def add_tile(tile, total):
        start = (tile * ROWS_DEV).astype(jnp.int32)
        older = lax.dynamic_slice_in_dim(stored_snapshots, start, ROWS_DEV, 1)
        fresh = lax.dynamic_slice_in_dim(sampled, tile.astype(jnp.int32), 1, 0)
        rows_f = jnp.concatenate([older, fresh], 0).astype(jnp.float32)
        return total + jnp.dot(rows_f, rows_f.T, precision=lax.Precision.HIGHEST)
    gram = lax.fori_loop(jnp.int32(0), jnp.int32(TILES), add_tile, jnp.zeros((SNAPS, SNAPS), jnp.float32))
    gram = gram / float(ROWS)
    snapshot_r = jnp.linalg.cholesky(gram).T
    return (new_fields, snapshot_r)
```

```python
import functools

import jax
import jax.numpy as jnp
from jax import lax
from jax.experimental import pallas as pl
from jax.experimental.pallas import tpu as pltpu
from jax.sharding import PartitionSpec as P

MESH = pl.DeviceIdType.MESH
SNAPS = 128
STRIDE = 32


def lanes(shape):
    return lax.broadcasted_iota(jnp.int32, shape, len(shape) - 1)


def rows(shape):
    return lax.broadcasted_iota(jnp.int32, shape, len(shape) - 2)


def step_kernel(
    sizes,
    u_hbm, k_hbm, v_hbm, s_hbm, idx_ref,
    new_hbm, gram_ref,
    u_pad, k_pad, vx_pad, vyz, snaps, new_vmem, hy_u, hy_v, hy_k, hz_send, hz, pick, chosen, column,
    pieces, parts, zparts, full, col_parts, col_zparts,
    load_sem, store_sem, halo_send, halo_recv, mat_send, mat_recv, zmat_send, zmat_recv,
    all_send, all_recv, col_send, col_recv, zcol_send, zcol_recv,
):
    nx, ny, nz = sizes
    plane = nx * ny
    cx, cy, cz = k_hbm.shape
    x, y, z = lax.axis_index("gx"), lax.axis_index("gy"), lax.axis_index("gz")
    me = x * ny + y

    loads = [
        pltpu.make_async_copy(s_hbm, snaps, load_sem.at[0]),
        pltpu.make_async_copy(u_hbm, u_pad.at[:, pl.ds(1, cx)], load_sem.at[1]),
        pltpu.make_async_copy(k_hbm, k_pad.at[pl.ds(1, cx)], load_sem.at[2]),
        pltpu.make_async_copy(v_hbm.at[0], vx_pad.at[pl.ds(1, cx)], load_sem.at[3]),
        pltpu.make_async_copy(v_hbm.at[pl.ds(1, 2)], vyz, load_sem.at[4]),
    ]
    for load in loads:
        load.start()

    def plane_peer(j):
        peer = lax.rem(me + j, plane)
        return peer, (lax.div(peer, ny), lax.rem(peer, ny), z)

    def line_peer(j):
        return (x, y, lax.rem(z + j, nz))

    barrier = pltpu.get_barrier_semaphore()

    def greet_plane(j, carry):
        pl.semaphore_signal(barrier, inc=1, device_id=plane_peer(j)[1], device_id_type=MESH)
        return carry

    def greet_line(j, carry):
        pl.semaphore_signal(barrier, inc=1, device_id=line_peer(j), device_id_type=MESH)
        return carry

    lax.fori_loop(1, plane, greet_plane, 0)
    lax.fori_loop(1, nz, greet_line, 0)

    loads[0].wait()
    block = snaps[...]
    gram = lax.dot_general(
        block, block, (((1,), (1,)), ((), ())), preferred_element_type=jnp.float32
    )
    gram_ref[...] = jnp.zeros_like(gram_ref)
    gram_ref[0:SNAPS - 1, 0:SNAPS - 1] = gram
    per = SNAPS // plane
    for i in range(plane):
        pieces[i] = gram_ref[i * per:(i + 1) * per]

    for load in loads[1:]:
        load.wait()
    lane = lanes((cy, cz))

    def pack_layer(i, faces):
        low, high = faces
        arrays = [u_pad[0, i + 1], u_pad[1, i + 1], u_pad[2, i + 1], vyz[1, i], k_pad[i + 1]]
        for a, values in enumerate(arrays):
            spot = a * cx + i
            low = jnp.where(lane == spot, pltpu.roll(values, spot, 1), low)
            high = jnp.where(lane == spot, pltpu.roll(values, spot + 1, 1), high)
        return low, high

    empty = jnp.zeros((cy, cz), jnp.float32)
    low, high = lax.fori_loop(0, cx, pack_layer, (empty, empty))
    hz_send[0] = low
    hz_send[1] = high

    pl.semaphore_wait(barrier, plane - 1 + nz - 1)

    def send(src, dst, side, number, device):
        return pltpu.make_async_remote_copy(
            src_ref=src, dst_ref=dst, send_sem=halo_send.at[side, number],
            recv_sem=halo_recv.at[side, number], device_id=device, device_id_type=MESH,
        )

    up_x, down_x = lax.rem(x + 1, nx), lax.rem(x + nx - 1, nx)
    up_y, down_y = lax.rem(y + 1, ny), lax.rem(y + ny - 1, ny)
    up_z, down_z = lax.rem(z + 1, nz), lax.rem(z + nz - 1, nz)
    halos = [
        send(hz_send.at[1], hz.at[0], 4, 0, (x, y, up_z)),
        send(hz_send.at[0], hz.at[1], 5, 0, (x, y, down_z)),
        send(u_hbm.at[:, cx - 1], u_pad.at[:, 0], 0, 0, (up_x, y, z)),
        send(v_hbm.at[0, cx - 1], vx_pad.at[0], 0, 1, (up_x, y, z)),
        send(k_hbm.at[cx - 1], k_pad.at[0], 0, 2, (up_x, y, z)),
        send(u_hbm.at[:, 0], u_pad.at[:, cx + 1], 1, 0, (down_x, y, z)),
        send(v_hbm.at[0, 0], vx_pad.at[cx + 1], 1, 1, (down_x, y, z)),
        send(k_hbm.at[0], k_pad.at[cx + 1], 1, 2, (down_x, y, z)),
        send(u_hbm.at[:, :, cy - 1], hy_u.at[0], 2, 0, (x, up_y, z)),
        send(v_hbm.at[1, :, cy - 1], hy_v.at[0], 2, 1, (x, up_y, z)),
        send(k_hbm.at[:, cy - 1], hy_k.at[0], 2, 2, (x, up_y, z)),
        send(u_hbm.at[:, :, 0], hy_u.at[1], 3, 0, (x, down_y, z)),
        send(v_hbm.at[1, :, 0], hy_v.at[1], 3, 1, (x, down_y, z)),
        send(k_hbm.at[:, 0], hy_k.at[1], 3, 2, (x, down_y, z)),
    ]
    for halo in halos:
        halo.start()

    def send_piece(j, carry):
        peer, device = plane_peer(j)
        pltpu.make_async_remote_copy(
            src_ref=pieces.at[peer], dst_ref=parts.at[me], send_sem=mat_send, recv_sem=mat_recv,
            device_id=device, device_id_type=MESH,
        ).start()
        return carry

    lax.fori_loop(1, plane, send_piece, 0)
    parts[me] = pieces[me]

    wide = lanes((cx * cy, cz))
    offset = (idx_ref[...] & (STRIDE - 1)).astype(jnp.float32)
    samples = cz // STRIDE
    group = cz // samples
    spread = jnp.broadcast_to(offset[:, None, :], (cx * cy // group, group, cz)).reshape(cx * cy, cz)
    own = lax.div(wide, samples) == lax.rem(rows((cx * cy, cz)), group)
    spread = jnp.where(own, spread, 0.0).astype(jnp.bfloat16)
    square = (cz, cz)
    to_cells = (lax.rem(rows(square), samples) == lax.div(lanes(square), STRIDE)).astype(jnp.bfloat16)
    at = jnp.dot(spread, to_cells, preferred_element_type=jnp.float32)
    hit = at.astype(jnp.int32) == lax.rem(wide, STRIDE)
    pick[...] = jnp.where(hit, 1.0, 0.0).reshape(cx, cy, cz)

    for halo in halos:
        halo.wait_recv()

    @pl.when(x == 0)
    def _():
        u_pad[:, 0] = jnp.zeros_like(u_pad[:, 0])
        vx_pad[0] = jnp.zeros_like(vx_pad[0])
        k_pad[0] = jnp.zeros_like(k_pad[0])

    @pl.when(x == nx - 1)
    def _():
        u_pad[:, cx + 1] = jnp.zeros_like(u_pad[:, cx + 1])
        vx_pad[cx + 1] = jnp.zeros_like(vx_pad[cx + 1])
        k_pad[cx + 1] = jnp.zeros_like(k_pad[cx + 1])

    @pl.when(y == 0)
    def _():
        hy_u[0] = jnp.zeros_like(hy_u[0])
        hy_v[0] = jnp.zeros_like(hy_v[0])
        hy_k[0] = jnp.zeros_like(hy_k[0])

    @pl.when(y == ny - 1)
    def _():
        hy_u[1] = jnp.zeros_like(hy_u[1])
        hy_v[1] = jnp.zeros_like(hy_v[1])
        hy_k[1] = jnp.zeros_like(hy_k[1])

    @pl.when(z == 0)
    def _():
        hz[0] = jnp.zeros_like(hz[0])

    @pl.when(z == nz - 1)
    def _():
        hz[1] = jnp.zeros_like(hz[1])

    row = rows((cy, cz))

    def step_layer(i, carry):
        z_low, z_high = hz[0], hz[1]

        def y_sides(values, below, above):
            plus = jnp.where(row == cy - 1, above, pltpu.roll(values, cy - 1, 0))
            minus = jnp.where(row == 0, below, pltpu.roll(values, 1, 0))
            return plus, minus

        def z_sides(values, a):
            spot = a * cx + i
            plus = jnp.where(
                lane == cz - 1, pltpu.roll(z_high, cz - 1 - spot, 1), pltpu.roll(values, cz - 1, 1)
            )
            minus = jnp.where(lane == 0, pltpu.roll(z_low, cz - spot, 1), pltpu.roll(values, 1, 1))
            return plus, minus

        center_k = k_pad[i + 1]
        k_sides = [
            (k_pad[i + 2], k_pad[i]),
            y_sides(center_k, hy_k[0, pl.ds(i, 1)], hy_k[1, pl.ds(i, 1)]),
            z_sides(center_k, 4),
        ]
        v_sides = [
            (vx_pad[i + 2], vx_pad[i]),
            y_sides(vyz[0, i], hy_v[0, pl.ds(i, 1)], hy_v[1, pl.ds(i, 1)]),
            z_sides(vyz[1, i], 3),
        ]
        faces = [(0.5 * (plus + center_k), 0.5 * (center_k + minus)) for plus, minus in k_sides]
        speeds = [(0.5 * plus, 0.5 * minus) for plus, minus in v_sides]
        marked = pick[i] > 0.5
        for f in range(3):
            center = u_pad[f, i + 1]
            u_sides = [
                (u_pad[f, i + 2], u_pad[f, i]),
                y_sides(center, hy_u[0, f, pl.ds(i, 1)], hy_u[1, f, pl.ds(i, 1)]),
                z_sides(center, f),
            ]
            terms = []
            for (k_up, k_down), (v_up, v_down), (plus, minus) in zip(faces, speeds, u_sides):
                terms.append(
                    k_up * (plus - center) - k_down * (center - minus) - (v_up * plus - v_down * minus)
                )
            fresh = center + (terms[0] + terms[1] + terms[2])
            new_vmem[f, i] = fresh
            chosen[f, i] = jnp.where(marked, fresh, 0.0).astype(jnp.bfloat16)
        return carry

    lax.fori_loop(0, cx, step_layer, 0)
    store = pltpu.make_async_copy(new_vmem, new_hbm, store_sem)
    store.start()

    spots = 3 * cx * cy
    by_row = jnp.dot(
        chosen[...].reshape(spots, cz),
        (lax.div(rows(square), STRIDE) == lax.rem(lanes(square), samples)).astype(jnp.bfloat16),
        preferred_element_type=jnp.float32,
    ).reshape(spots // group, group, cz)
    own = lax.div(lanes((1, group, cz)), samples) == rows((1, group, cz))
    fresh_rows = jnp.sum(jnp.where(own, by_row, 0.0), axis=1)
    column[...] = jnp.zeros_like(column)
    for i in range(spots // group):
        column[0:1, i * cz:(i + 1) * cz] = fresh_rows[i:i + 1]
    line = lax.dot_general(
        column[...].astype(jnp.bfloat16), snaps[...], (((1,), (1,)), ((), ())),
        preferred_element_type=jnp.float32,
    )
    own_square = jnp.sum(jnp.sum(fresh_rows * fresh_rows, axis=0, keepdims=True), axis=1, keepdims=True)
    last = lanes((1, SNAPS)) == SNAPS - 1
    column[:, 0:SNAPS - 1] = line
    col_parts[me] = jnp.where(last, own_square, column[0:1, 0:SNAPS])

    def send_column(j, carry):
        peer, device = plane_peer(j)
        pltpu.make_async_remote_copy(
            src_ref=col_parts.at[me], dst_ref=col_parts.at[me], send_sem=col_send, recv_sem=col_recv,
            device_id=device, device_id_type=MESH,
        ).start()
        return carry

    lax.fori_loop(1, plane, send_column, 0)

    def arrived(ref, sem, count):
        pltpu.make_async_copy(ref.at[pl.ds(0, count)], ref.at[pl.ds(0, count)], sem).wait()

    arrived(parts, mat_recv, plane - 1)
    zparts[z] = jnp.sum(parts[...], axis=0)

    def send_sum(j, carry):
        pltpu.make_async_remote_copy(
            src_ref=zparts.at[z], dst_ref=zparts.at[z], send_sem=zmat_send, recv_sem=zmat_recv,
            device_id=line_peer(j), device_id_type=MESH,
        ).start()
        return carry

    lax.fori_loop(1, nz, send_sum, 0)

    arrived(col_parts, col_recv, plane - 1)
    col_zparts[z] = jnp.sum(col_parts[...], axis=0)

    def send_column_sum(j, carry):
        pltpu.make_async_remote_copy(
            src_ref=col_zparts.at[z], dst_ref=col_zparts.at[z], send_sem=zcol_send, recv_sem=zcol_recv,
            device_id=line_peer(j), device_id_type=MESH,
        ).start()
        return carry

    lax.fori_loop(1, nz, send_column_sum, 0)

    arrived(zparts, zmat_recv, nz - 1)
    full[me] = jnp.sum(zparts[...], axis=0)

    def send_total(j, carry):
        peer, device = plane_peer(j)
        pltpu.make_async_remote_copy(
            src_ref=full.at[me], dst_ref=full.at[me], send_sem=all_send, recv_sem=all_recv,
            device_id=device, device_id_type=MESH,
        ).start()
        return carry

    lax.fori_loop(1, plane, send_total, 0)

    arrived(col_zparts, zcol_recv, nz - 1)
    total_column = jnp.sum(col_zparts[...], axis=0)
    arrived(full, all_recv, plane - 1)

    scale = 1.0 / (SNAPS // SNAPS * s_hbm.shape[1] * plane * nz)
    for i in range(plane):
        gram_ref[i * per:(i + 1) * per] = full[i] * scale
    gram_ref[SNAPS - 1:SNAPS] = total_column * scale

    store.wait()
    for halo in halos:
        halo.wait_send()
    arrived(pieces, mat_send, plane - 1)
    arrived(zparts, zmat_send, nz - 1)
    arrived(full, all_send, plane - 1)
    arrived(col_parts, col_send, plane - 1)
    arrived(col_zparts, zcol_send, nz - 1)


def per_device(sizes, fields, diffusivity, velocity, stored_snapshots, sample_index):
    nx, ny, nz = sizes
    plane = nx * ny
    _, cx, cy, cz = fields.shape
    per = SNAPS // plane
    f32, dma = jnp.float32, pltpu.SemaphoreType.DMA
    anywhere = pl.BlockSpec(memory_space=pl.ANY)
    vmem = pl.BlockSpec(memory_space=pltpu.VMEM)
    index = sample_index.reshape(-1, cz)
    new_fields, gram = pl.pallas_call(
        functools.partial(step_kernel, sizes),
        out_shape=(
            jax.ShapeDtypeStruct(fields.shape, f32),
            jax.ShapeDtypeStruct((SNAPS, SNAPS), f32),
        ),
        in_specs=[anywhere] * 4 + [vmem],
        out_specs=(anywhere, vmem),
        scratch_shapes=[
            pltpu.VMEM((3, cx + 2, cy, cz), f32),
            pltpu.VMEM((cx + 2, cy, cz), f32),
            pltpu.VMEM((cx + 2, cy, cz), f32),
            pltpu.VMEM((2, cx, cy, cz), f32),
            pltpu.VMEM(stored_snapshots.shape, jnp.bfloat16),
            pltpu.VMEM((3, cx, cy, cz), f32),
            pltpu.VMEM((2, 3, cx, cz), f32),
            pltpu.VMEM((2, cx, cz), f32),
            pltpu.VMEM((2, cx, cz), f32),
            pltpu.VMEM((2, cy, cz), f32),
            pltpu.VMEM((2, cy, cz), f32),
            pltpu.VMEM((cx, cy, cz), f32),
            pltpu.VMEM((3, cx, cy, cz), jnp.bfloat16),
            pltpu.VMEM((8, stored_snapshots.shape[1]), f32),
            pltpu.VMEM((plane, per, SNAPS), f32),
            pltpu.VMEM((plane, per, SNAPS), f32),
            pltpu.VMEM((nz, per, SNAPS), f32),
            pltpu.VMEM((plane, per, SNAPS), f32),
            pltpu.VMEM((plane, 1, SNAPS), f32),
            pltpu.VMEM((nz, 1, SNAPS), f32),
            dma((5,)),
            dma,
            dma((6, 3)),
            dma((6, 3)),
        ] + [dma] * 10,
        compiler_params=pltpu.CompilerParams(collective_id=0, has_side_effects=True),
        name="step",
    )(fields, diffusivity, velocity, stored_snapshots, index)
    snapshot_r = lax.linalg.cholesky(gram, symmetrize_input=False).T
    return (new_fields, snapshot_r)


def solution(mesh):
    sizes = tuple(mesh.shape[axis] for axis in ("gx", "gy", "gz"))
    placed = (
        P(None, "gx", "gy", "gz"),
        P("gx", "gy", "gz"),
        P(None, "gx", "gy", "gz"),
        P(None, ("gx", "gy", "gz")),
        P(("gx", "gy", "gz")),
    )
    return jax.shard_map(
        functools.partial(per_device, sizes),
        mesh=mesh,
        in_specs=placed,
        out_specs=(P(None, "gx", "gy", "gz"), P()),
        check_vma=False,
    )
```

```python
import functools

import jax
import jax.numpy as jnp
from jax import lax
from jax.experimental import pallas as pl
from jax.experimental.pallas import tpu as pltpu
from jax.sharding import PartitionSpec as P

MESH = pl.DeviceIdType.MESH
SNAPS = 128
STRIDE = 32


def lanes(shape):
    return lax.broadcasted_iota(jnp.int32, shape, len(shape) - 1)


def rows(shape):
    return lax.broadcasted_iota(jnp.int32, shape, len(shape) - 2)


def step_kernel(
    sizes,
    u_hbm, k_hbm, v_hbm, s_hbm, idx_ref,
    new_hbm, gram_ref,
    u_pad, k_pad, vx_pad, vyz, snaps, new_vmem, hy_u, hy_v, hy_k, hz_send, hz, pick, chosen, column,
    pieces, parts, zparts, full, col_parts, col_zparts,
    load_sem, store_sem, halo_send, halo_recv, mat_send, mat_recv, zmat_send, zmat_recv,
    all_send, all_recv, col_send, col_recv, zcol_send, zcol_recv,
):
    nx, ny, nz = sizes
    plane = nx * ny
    cx, cy, cz = k_hbm.shape
    x, y, z = lax.axis_index("gx"), lax.axis_index("gy"), lax.axis_index("gz")
    me = x * ny + y

    loads = [
        pltpu.make_async_copy(s_hbm, snaps, load_sem.at[0]),
        pltpu.make_async_copy(u_hbm, u_pad.at[:, pl.ds(1, cx)], load_sem.at[1]),
        pltpu.make_async_copy(k_hbm, k_pad.at[pl.ds(1, cx)], load_sem.at[2]),
        pltpu.make_async_copy(v_hbm.at[0], vx_pad.at[pl.ds(1, cx)], load_sem.at[3]),
        pltpu.make_async_copy(v_hbm.at[pl.ds(1, 2)], vyz, load_sem.at[4]),
    ]
    for load in loads:
        load.start()

    def plane_peer(j):
        peer = lax.rem(me + j, plane)
        return peer, (lax.div(peer, ny), lax.rem(peer, ny), z)

    def line_peer(j):
        return (x, y, lax.rem(z + j, nz))

    barrier = pltpu.get_barrier_semaphore()

    def greet_plane(j, carry):
        pl.semaphore_signal(barrier, inc=1, device_id=plane_peer(j)[1], device_id_type=MESH)
        return carry

    def greet_line(j, carry):
        pl.semaphore_signal(barrier, inc=1, device_id=line_peer(j), device_id_type=MESH)
        return carry

    lax.fori_loop(1, plane, greet_plane, 0)
    lax.fori_loop(1, nz, greet_line, 0)

    loads[0].wait()
    block = snaps[...]
    gram = lax.dot_general(
        block, block, (((1,), (1,)), ((), ())), preferred_element_type=jnp.float32
    )
    gram_ref[...] = jnp.zeros_like(gram_ref)
    gram_ref[0:SNAPS - 1, 0:SNAPS - 1] = gram
    per = SNAPS // plane
    for i in range(plane):
        pieces[i] = gram_ref[i * per:(i + 1) * per]

    for load in loads[1:]:
        load.wait()
    lane = lanes((cy, cz))

    def pack_layer(i, faces):
        low, high = faces
        arrays = [u_pad[0, i + 1], u_pad[1, i + 1], u_pad[2, i + 1], vyz[1, i], k_pad[i + 1]]
        for a, values in enumerate(arrays):
            spot = a * cx + i
            low = jnp.where(lane == spot, pltpu.roll(values, spot, 1), low)
            high = jnp.where(lane == spot, pltpu.roll(values, spot + 1, 1), high)
        return low, high

    empty = jnp.zeros((cy, cz), jnp.float32)
    low, high = lax.fori_loop(0, cx, pack_layer, (empty, empty))
    hz_send[0] = low
    hz_send[1] = high

    pl.semaphore_wait(barrier, plane - 1 + nz - 1)

    def send(src, dst, side, number, device):
        return pltpu.make_async_remote_copy(
            src_ref=src, dst_ref=dst, send_sem=halo_send.at[side, number],
            recv_sem=halo_recv.at[side, number], device_id=device, device_id_type=MESH,
        )

    up_x, down_x = lax.rem(x + 1, nx), lax.rem(x + nx - 1, nx)
    up_y, down_y = lax.rem(y + 1, ny), lax.rem(y + ny - 1, ny)
    up_z, down_z = lax.rem(z + 1, nz), lax.rem(z + nz - 1, nz)
    halos = [
        send(hz_send.at[1], hz.at[0], 4, 0, (x, y, up_z)),
        send(hz_send.at[0], hz.at[1], 5, 0, (x, y, down_z)),
        send(u_hbm.at[:, cx - 1], u_pad.at[:, 0], 0, 0, (up_x, y, z)),
        send(v_hbm.at[0, cx - 1], vx_pad.at[0], 0, 1, (up_x, y, z)),
        send(k_hbm.at[cx - 1], k_pad.at[0], 0, 2, (up_x, y, z)),
        send(u_hbm.at[:, 0], u_pad.at[:, cx + 1], 1, 0, (down_x, y, z)),
        send(v_hbm.at[0, 0], vx_pad.at[cx + 1], 1, 1, (down_x, y, z)),
        send(k_hbm.at[0], k_pad.at[cx + 1], 1, 2, (down_x, y, z)),
        send(u_hbm.at[:, :, cy - 1], hy_u.at[0], 2, 0, (x, up_y, z)),
        send(v_hbm.at[1, :, cy - 1], hy_v.at[0], 2, 1, (x, up_y, z)),
        send(k_hbm.at[:, cy - 1], hy_k.at[0], 2, 2, (x, up_y, z)),
        send(u_hbm.at[:, :, 0], hy_u.at[1], 3, 0, (x, down_y, z)),
        send(v_hbm.at[1, :, 0], hy_v.at[1], 3, 1, (x, down_y, z)),
        send(k_hbm.at[:, 0], hy_k.at[1], 3, 2, (x, down_y, z)),
    ]
    for halo in halos:
        halo.start()

    def send_piece(j, carry):
        peer, device = plane_peer(j)
        pltpu.make_async_remote_copy(
            src_ref=pieces.at[peer], dst_ref=parts.at[me], send_sem=mat_send, recv_sem=mat_recv,
            device_id=device, device_id_type=MESH,
        ).start()
        return carry

    lax.fori_loop(1, plane, send_piece, 0)
    parts[me] = pieces[me]

    wide = lanes((cx * cy, cz))
    offset = (idx_ref[...] & (STRIDE - 1)).astype(jnp.float32)
    samples = cz // STRIDE
    group = cz // samples
    spread = jnp.broadcast_to(offset[:, None, :], (cx * cy // group, group, cz)).reshape(cx * cy, cz)
    own = lax.div(wide, samples) == lax.rem(rows((cx * cy, cz)), group)
    spread = jnp.where(own, spread, 0.0).astype(jnp.bfloat16)
    square = (cz, cz)
    to_cells = (lax.rem(rows(square), samples) == lax.div(lanes(square), STRIDE)).astype(jnp.bfloat16)
    at = jnp.dot(spread, to_cells, preferred_element_type=jnp.float32)
    hit = at.astype(jnp.int32) == lax.rem(wide, STRIDE)
    pick[...] = jnp.where(hit, 1.0, 0.0).reshape(cx, cy, cz)

    for halo in halos:
        halo.wait_recv()

    @pl.when(x == 0)
    def _():
        u_pad[:, 0] = jnp.zeros_like(u_pad[:, 0])
        vx_pad[0] = jnp.zeros_like(vx_pad[0])
        k_pad[0] = jnp.zeros_like(k_pad[0])

    @pl.when(x == nx - 1)
    def _():
        u_pad[:, cx + 1] = jnp.zeros_like(u_pad[:, cx + 1])
        vx_pad[cx + 1] = jnp.zeros_like(vx_pad[cx + 1])
        k_pad[cx + 1] = jnp.zeros_like(k_pad[cx + 1])

    @pl.when(y == 0)
    def _():
        hy_u[0] = jnp.zeros_like(hy_u[0])
        hy_v[0] = jnp.zeros_like(hy_v[0])
        hy_k[0] = jnp.zeros_like(hy_k[0])

    @pl.when(y == ny - 1)
    def _():
        hy_u[1] = jnp.zeros_like(hy_u[1])
        hy_v[1] = jnp.zeros_like(hy_v[1])
        hy_k[1] = jnp.zeros_like(hy_k[1])

    @pl.when(z == 0)
    def _():
        hz[0] = jnp.zeros_like(hz[0])

    @pl.when(z == nz - 1)
    def _():
        hz[1] = jnp.zeros_like(hz[1])

    row = rows((cy, cz))

    def step_layer(i, carry):
        z_low, z_high = hz[0], hz[1]

        def y_sides(values, below, above):
            plus = jnp.where(row == cy - 1, above, pltpu.roll(values, cy - 1, 0))
            minus = jnp.where(row == 0, below, pltpu.roll(values, 1, 0))
            return plus, minus

        def z_sides(values, a):
            spot = a * cx + i
            plus = jnp.where(
                lane == cz - 1, pltpu.roll(z_high, cz - 1 - spot, 1), pltpu.roll(values, cz - 1, 1)
            )
            minus = jnp.where(lane == 0, pltpu.roll(z_low, cz - spot, 1), pltpu.roll(values, 1, 1))
            return plus, minus

        center_k = k_pad[i + 1]
        k_sides = [
            (k_pad[i + 2], k_pad[i]),
            y_sides(center_k, hy_k[0, pl.ds(i, 1)], hy_k[1, pl.ds(i, 1)]),
            z_sides(center_k, 4),
        ]
        v_sides = [
            (vx_pad[i + 2], vx_pad[i]),
            y_sides(vyz[0, i], hy_v[0, pl.ds(i, 1)], hy_v[1, pl.ds(i, 1)]),
            z_sides(vyz[1, i], 3),
        ]
        faces = [(0.5 * (plus + center_k), 0.5 * (center_k + minus)) for plus, minus in k_sides]
        speeds = [(0.5 * plus, 0.5 * minus) for plus, minus in v_sides]
        marked = pick[i] > 0.5
        for f in range(3):
            center = u_pad[f, i + 1]
            u_sides = [
                (u_pad[f, i + 2], u_pad[f, i]),
                y_sides(center, hy_u[0, f, pl.ds(i, 1)], hy_u[1, f, pl.ds(i, 1)]),
                z_sides(center, f),
            ]
            terms = []
            for (k_up, k_down), (v_up, v_down), (plus, minus) in zip(faces, speeds, u_sides):
                terms.append(
                    k_up * (plus - center) - k_down * (center - minus) - (v_up * plus - v_down * minus)
                )
            fresh = center + (terms[0] + terms[1] + terms[2])
            new_vmem[f, i] = fresh
            chosen[f, i] = jnp.where(marked, fresh, 0.0).astype(jnp.bfloat16)
        return carry

    lax.fori_loop(0, cx, step_layer, 0)
    store = pltpu.make_async_copy(new_vmem, new_hbm, store_sem)
    store.start()

    spots = 3 * cx * cy
    by_row = jnp.dot(
        chosen[...].reshape(spots, cz),
        (lax.div(rows(square), STRIDE) == lax.rem(lanes(square), samples)).astype(jnp.bfloat16),
        preferred_element_type=jnp.float32,
    ).reshape(spots // group, group, cz)
    own = lax.div(lanes((1, group, cz)), samples) == rows((1, group, cz))
    fresh_rows = jnp.sum(jnp.where(own, by_row, 0.0), axis=1)
    column[...] = jnp.zeros_like(column)
    for i in range(spots // group):
        column[0:1, i * cz:(i + 1) * cz] = fresh_rows[i:i + 1]
    line = lax.dot_general(
        column[...].astype(jnp.bfloat16), snaps[...], (((1,), (1,)), ((), ())),
        preferred_element_type=jnp.float32,
    )
    own_square = jnp.sum(jnp.sum(fresh_rows * fresh_rows, axis=0, keepdims=True), axis=1, keepdims=True)
    last = lanes((1, SNAPS)) == SNAPS - 1
    column[:, 0:SNAPS - 1] = line
    col_parts[me] = jnp.where(last, own_square, column[0:1, 0:SNAPS])

    def send_column(j, carry):
        peer, device = plane_peer(j)
        pltpu.make_async_remote_copy(
            src_ref=col_parts.at[me], dst_ref=col_parts.at[me], send_sem=col_send, recv_sem=col_recv,
            device_id=device, device_id_type=MESH,
        ).start()
        return carry

    lax.fori_loop(1, plane, send_column, 0)

    def arrived(ref, sem, count):
        pltpu.make_async_copy(ref.at[pl.ds(0, count)], ref.at[pl.ds(0, count)], sem).wait()

    arrived(parts, mat_recv, plane - 1)
    zparts[z] = jnp.sum(parts[...], axis=0)

    def send_sum(j, carry):
        pltpu.make_async_remote_copy(
            src_ref=zparts.at[z], dst_ref=zparts.at[z], send_sem=zmat_send, recv_sem=zmat_recv,
            device_id=line_peer(j), device_id_type=MESH,
        ).start()
        return carry

    lax.fori_loop(1, nz, send_sum, 0)

    arrived(col_parts, col_recv, plane - 1)
    col_zparts[z] = jnp.sum(col_parts[...], axis=0)

    def send_column_sum(j, carry):
        pltpu.make_async_remote_copy(
            src_ref=col_zparts.at[z], dst_ref=col_zparts.at[z], send_sem=zcol_send, recv_sem=zcol_recv,
            device_id=line_peer(j), device_id_type=MESH,
        ).start()
        return carry

    lax.fori_loop(1, nz, send_column_sum, 0)

    arrived(zparts, zmat_recv, nz - 1)
    full[me] = jnp.sum(zparts[...], axis=0)

    def send_total(j, carry):
        peer, device = plane_peer(j)
        pltpu.make_async_remote_copy(
            src_ref=full.at[me], dst_ref=full.at[me], send_sem=all_send, recv_sem=all_recv,
            device_id=device, device_id_type=MESH,
        ).start()
        return carry

    lax.fori_loop(1, plane, send_total, 0)

    arrived(col_zparts, zcol_recv, nz - 1)
    total_column = jnp.sum(col_zparts[...], axis=0)
    arrived(full, all_recv, plane - 1)

    scale = 1.0 / (SNAPS // SNAPS * s_hbm.shape[1] * plane * nz)
    for i in range(plane):
        gram_ref[i * per:(i + 1) * per] = full[i] * scale
    gram_ref[SNAPS - 1:SNAPS] = total_column * scale

    store.wait()
    for halo in halos:
        halo.wait_send()
    arrived(pieces, mat_send, plane - 1)
    arrived(zparts, zmat_send, nz - 1)
    arrived(full, all_send, plane - 1)
    arrived(col_parts, col_send, plane - 1)
    arrived(col_zparts, zcol_send, nz - 1)


def factor_kernel(gram_ref, new_in, r_ref, new_out, held, sem_in, sem_out):
    size, edge = gram_ref.shape[0], 8
    blocks = size // edge
    tile = (edge, size)
    fetch = pltpu.make_async_copy(new_in, held, sem_in)
    keep = pltpu.make_async_copy(held, new_out, sem_out)
    fetch.start()

    last_lane = lanes(tile) == size - 1
    turned = jnp.transpose(gram_ref[size - edge:size])
    work = [
        jnp.where(last_lane, turned[t * edge:(t + 1) * edge, edge - 1:edge], gram_ref[t * edge:(t + 1) * edge])
        for t in range(blocks)
    ]

    def spread_lane(values, at):
        return jnp.broadcast_to(values[:, at:at + 1], tile)

    for b in range(blocks):
        if b == 2:
            fetch.wait()
            keep.start()
        base = b * edge
        line = [jnp.broadcast_to(work[b][i:i + 1], tile) for i in range(edge)]
        entry = [
            [spread_lane(line[i], base + j) if j >= i else None for j in range(edge)]
            for i in range(edge)
        ]
        ahead = b + 1 < blocks
        if ahead:
            following = work[b + 1]
            side = [spread_lane(following, base + i) for i in range(edge)]
        ratio_lines = []
        for i in range(edge):
            inverse = pl.reciprocal(entry[i][i], approx=False)
            ratio = [entry[i][j] * inverse if j > i else None for j in range(edge)]
            ratio_line = line[i] * inverse
            ratio_lines.append(ratio_line)
            for j in range(i + 1, edge):
                for k in range(j, edge):
                    entry[j][k] = entry[j][k] - ratio[j] * entry[i][k]
            for j in range(i + 1, edge):
                line[j] = line[j] - ratio[j] * line[i]
            if ahead:
                following = following - side[i] * ratio_line
                for j in range(i + 1, edge):
                    side[j] = side[j] - ratio[j] * side[i]
        sub = rows(tile)
        panel, ratios = line[0], ratio_lines[0]
        root = lax.rsqrt(entry[0][0])
        for i in range(1, edge):
            panel = jnp.where(sub == i, line[i], panel)
            ratios = jnp.where(sub == i, ratio_lines[i], ratios)
            root = jnp.where(sub == i, lax.rsqrt(entry[i][i]), root)
        r_ref[base:base + edge] = jnp.where(lanes(tile) >= sub + base, panel * root, 0.0)
        if ahead:
            work[b + 1] = following
        if b + 2 < blocks:
            flipped = jnp.transpose(ratios)
            for t in range(b + 2, blocks):
                chunk = flipped[t * edge:(t + 1) * edge]
                value = work[t]
                for i in range(edge):
                    value = value - jnp.broadcast_to(chunk[:, i:i + 1], tile) * line[i]
                work[t] = value
    keep.wait()


def per_device(sizes, fields, diffusivity, velocity, stored_snapshots, sample_index):
    nx, ny, nz = sizes
    plane = nx * ny
    _, cx, cy, cz = fields.shape
    per = SNAPS // plane
    f32, dma = jnp.float32, pltpu.SemaphoreType.DMA
    anywhere = pl.BlockSpec(memory_space=pl.ANY)
    vmem = pl.BlockSpec(memory_space=pltpu.VMEM)
    index = sample_index.reshape(-1, cz)
    new_fields, gram = pl.pallas_call(
        functools.partial(step_kernel, sizes),
        out_shape=(
            jax.ShapeDtypeStruct(fields.shape, f32),
            jax.ShapeDtypeStruct((SNAPS, SNAPS), f32),
        ),
        in_specs=[anywhere] * 4 + [vmem],
        out_specs=(anywhere, vmem),
        scratch_shapes=[
            pltpu.VMEM((3, cx + 2, cy, cz), f32),
            pltpu.VMEM((cx + 2, cy, cz), f32),
            pltpu.VMEM((cx + 2, cy, cz), f32),
            pltpu.VMEM((2, cx, cy, cz), f32),
            pltpu.VMEM(stored_snapshots.shape, jnp.bfloat16),
            pltpu.VMEM((3, cx, cy, cz), f32),
            pltpu.VMEM((2, 3, cx, cz), f32),
            pltpu.VMEM((2, cx, cz), f32),
            pltpu.VMEM((2, cx, cz), f32),
            pltpu.VMEM((2, cy, cz), f32),
            pltpu.VMEM((2, cy, cz), f32),
            pltpu.VMEM((cx, cy, cz), f32),
            pltpu.VMEM((3, cx, cy, cz), jnp.bfloat16),
            pltpu.VMEM((8, stored_snapshots.shape[1]), f32),
            pltpu.VMEM((plane, per, SNAPS), f32),
            pltpu.VMEM((plane, per, SNAPS), f32),
            pltpu.VMEM((nz, per, SNAPS), f32),
            pltpu.VMEM((plane, per, SNAPS), f32),
            pltpu.VMEM((plane, 1, SNAPS), f32),
            pltpu.VMEM((nz, 1, SNAPS), f32),
            dma((5,)),
            dma,
            dma((6, 3)),
            dma((6, 3)),
        ] + [dma] * 10,
        compiler_params=pltpu.CompilerParams(collective_id=0, has_side_effects=True),
        name="step",
    )(fields, diffusivity, velocity, stored_snapshots, index)
    snapshot_r, new_fields = pl.pallas_call(
        factor_kernel,
        out_shape=(
            jax.ShapeDtypeStruct((SNAPS, SNAPS), f32),
            jax.ShapeDtypeStruct(fields.shape, f32),
        ),
        in_specs=[vmem, anywhere],
        out_specs=(vmem, anywhere),
        scratch_shapes=[pltpu.VMEM(fields.shape, f32), dma, dma],
        name="factor",
    )(gram, new_fields)
    return (new_fields, snapshot_r)


def solution(mesh):
    sizes = tuple(mesh.shape[axis] for axis in ("gx", "gy", "gz"))
    placed = (
        P(None, "gx", "gy", "gz"),
        P("gx", "gy", "gz"),
        P(None, "gx", "gy", "gz"),
        P(None, ("gx", "gy", "gz")),
        P(("gx", "gy", "gz")),
    )
    return jax.shard_map(
        functools.partial(per_device, sizes),
        mesh=mesh,
        in_specs=placed,
        out_specs=(P(None, "gx", "gy", "gz"), P()),
        check_vma=False,
    )
```

```python
import functools

import jax
import jax.numpy as jnp
from jax import lax
from jax.experimental import pallas as pl
from jax.experimental.pallas import tpu as pltpu
from jax.sharding import PartitionSpec as P

MESH = pl.DeviceIdType.MESH
SNAPS = 128
UNROLL = 4
STRIDE = 32


def lanes(shape):
    return lax.broadcasted_iota(jnp.int32, shape, len(shape) - 1)


def rows(shape):
    return lax.broadcasted_iota(jnp.int32, shape, len(shape) - 2)


def step_kernel(
    sizes,
    u_hbm, k_hbm, v_hbm, s_hbm, idx_hbm,
    new_hbm, gram_ref,
    idx_ref, u_pad, k_pad, vx_pad, vyz, snaps, new_vmem, hy_u, hy_v, hy_k, hz_send, hz, pick, chosen, column,
    pieces, parts, zparts, full, col_parts, col_zparts,
    load_sem, store_sem, halo_send, halo_recv, mat_send, mat_recv, zmat_send, zmat_recv,
    all_send, all_recv, col_send, col_recv, zcol_send, zcol_recv,
):
    nx, ny, nz = sizes
    plane = nx * ny
    cx, cy, cz = k_hbm.shape
    x, y, z = lax.axis_index("gx"), lax.axis_index("gy"), lax.axis_index("gz")
    me = x * ny + y

    loads = [
        pltpu.make_async_copy(s_hbm, snaps, load_sem.at[0]),
        pltpu.make_async_copy(u_hbm, u_pad.at[:, pl.ds(1, cx)], load_sem.at[1]),
        pltpu.make_async_copy(k_hbm, k_pad.at[pl.ds(1, cx)], load_sem.at[2]),
        pltpu.make_async_copy(v_hbm.at[0], vx_pad.at[pl.ds(1, cx)], load_sem.at[3]),
        pltpu.make_async_copy(v_hbm.at[pl.ds(1, 2)], vyz, load_sem.at[4]),
        pltpu.make_async_copy(idx_hbm, idx_ref, load_sem.at[5]),
    ]
    for load in loads:
        load.start()

    near_x = [lax.rem(x + j, nx) for j in range(nx)]
    near_y = [lax.rem(y + j, ny) for j in range(ny)]
    plane_peers = [(px, py) for px in near_x for py in near_y][1:]
    line_peers = [lax.rem(z + j, nz) for j in range(1, nz)]

    barrier = pltpu.get_barrier_semaphore()
    for peer in plane_peers:
        pl.semaphore_signal(barrier, inc=1, device_id=(*peer, z), device_id_type=MESH)
    for peer in line_peers:
        pl.semaphore_signal(barrier, inc=1, device_id=(x, y, peer), device_id_type=MESH)

    def to_plane(src, dst, send_sem, recv_sem):
        for peer in plane_peers:
            pltpu.make_async_remote_copy(
                src_ref=src(peer), dst_ref=dst, send_sem=send_sem, recv_sem=recv_sem,
                device_id=(*peer, z), device_id_type=MESH,
            ).start()

    def to_line(ref, send_sem, recv_sem):
        for peer in line_peers:
            pltpu.make_async_remote_copy(
                src_ref=ref.at[z], dst_ref=ref.at[z], send_sem=send_sem, recv_sem=recv_sem,
                device_id=(x, y, peer), device_id_type=MESH,
            ).start()

    def arrived(ref, sem, count):
        pltpu.make_async_copy(ref.at[pl.ds(0, count)], ref.at[pl.ds(0, count)], sem).wait()

    loads[0].wait()
    block = snaps[...]
    gram = lax.dot_general(
        block, block, (((1,), (1,)), ((), ())), preferred_element_type=jnp.float32
    )
    gram_ref[...] = jnp.zeros_like(gram_ref)
    gram_ref[0:SNAPS - 1, 0:SNAPS - 1] = gram
    per = SNAPS // plane
    for i in range(plane):
        pieces[i] = gram_ref[i * per:(i + 1) * per]

    for load in loads[1:]:
        load.wait()
    lane = lanes((cy, cz))

    low = high = jnp.zeros((cy, cz), jnp.float32)
    for i in range(cx):
        arrays = [u_pad[0, i + 1], u_pad[1, i + 1], u_pad[2, i + 1], vyz[1, i], k_pad[i + 1]]
        for a, values in enumerate(arrays):
            spot = a * cx + i
            here = lane == spot
            low = jnp.where(here, pltpu.roll(values, spot, 1) if spot else values, low)
            high = jnp.where(here, pltpu.roll(values, spot + 1, 1), high)
    hz_send[0] = low
    hz_send[1] = high

    wide = lanes((cx * cy, cz))
    offset = (idx_ref[...] & (STRIDE - 1)).astype(jnp.float32)
    samples = cz // STRIDE
    group = cz // samples
    spread = jnp.broadcast_to(offset[:, None, :], (cx * cy // group, group, cz)).reshape(cx * cy, cz)
    own = lax.div(wide, samples) == lax.rem(rows((cx * cy, cz)), group)
    spread = jnp.where(own, spread, 0.0).astype(jnp.bfloat16)
    square = (cz, cz)
    to_cells = (lax.rem(rows(square), samples) == lax.div(lanes(square), STRIDE)).astype(jnp.bfloat16)
    at = jnp.dot(spread, to_cells, preferred_element_type=jnp.float32)
    hit = at.astype(jnp.int32) == lax.rem(wide, STRIDE)
    pick[...] = jnp.where(hit, 1.0, 0.0).reshape(cx, cy, cz)
    pl.semaphore_wait(barrier, plane - 1 + nz - 1)

    to_plane(lambda peer: pieces.at[peer[0] * ny + peer[1]], parts.at[me], mat_send, mat_recv)
    parts[me] = pieces[me]

    def send(src, dst, side, number, target):
        return pltpu.make_async_remote_copy(
            src_ref=src, dst_ref=dst, send_sem=halo_send.at[side, number],
            recv_sem=halo_recv.at[side, number], device_id=target, device_id_type=MESH,
        )

    up_x, down_x = lax.rem(x + 1, nx), lax.rem(x + nx - 1, nx)
    up_y, down_y = lax.rem(y + 1, ny), lax.rem(y + ny - 1, ny)
    up_z, down_z = lax.rem(z + 1, nz), lax.rem(z + nz - 1, nz)
    halos = [
        send(hz_send.at[1], hz.at[0], 4, 0, (x, y, up_z)),
        send(hz_send.at[0], hz.at[1], 5, 0, (x, y, down_z)),
        send(u_hbm.at[:, cx - 1], u_pad.at[:, 0], 0, 0, (up_x, y, z)),
        send(v_hbm.at[0, cx - 1], vx_pad.at[0], 0, 1, (up_x, y, z)),
        send(k_hbm.at[cx - 1], k_pad.at[0], 0, 2, (up_x, y, z)),
        send(u_hbm.at[:, 0], u_pad.at[:, cx + 1], 1, 0, (down_x, y, z)),
        send(v_hbm.at[0, 0], vx_pad.at[cx + 1], 1, 1, (down_x, y, z)),
        send(k_hbm.at[0], k_pad.at[cx + 1], 1, 2, (down_x, y, z)),
        send(u_hbm.at[:, :, cy - 1], hy_u.at[0], 2, 0, (x, up_y, z)),
        send(v_hbm.at[1, :, cy - 1], hy_v.at[0], 2, 1, (x, up_y, z)),
        send(k_hbm.at[:, cy - 1], hy_k.at[0], 2, 2, (x, up_y, z)),
        send(u_hbm.at[:, :, 0], hy_u.at[1], 3, 0, (x, down_y, z)),
        send(v_hbm.at[1, :, 0], hy_v.at[1], 3, 1, (x, down_y, z)),
        send(k_hbm.at[:, 0], hy_k.at[1], 3, 2, (x, down_y, z)),
    ]
    for halo in halos:
        halo.start()

    for halo in halos:
        halo.wait_recv()

    @pl.when(x == 0)
    def _():
        u_pad[:, 0] = jnp.zeros_like(u_pad[:, 0])
        vx_pad[0] = jnp.zeros_like(vx_pad[0])
        k_pad[0] = jnp.zeros_like(k_pad[0])

    @pl.when(x == nx - 1)
    def _():
        u_pad[:, cx + 1] = jnp.zeros_like(u_pad[:, cx + 1])
        vx_pad[cx + 1] = jnp.zeros_like(vx_pad[cx + 1])
        k_pad[cx + 1] = jnp.zeros_like(k_pad[cx + 1])

    @pl.when(y == 0)
    def _():
        hy_u[0] = jnp.zeros_like(hy_u[0])
        hy_v[0] = jnp.zeros_like(hy_v[0])
        hy_k[0] = jnp.zeros_like(hy_k[0])

    @pl.when(y == ny - 1)
    def _():
        hy_u[1] = jnp.zeros_like(hy_u[1])
        hy_v[1] = jnp.zeros_like(hy_v[1])
        hy_k[1] = jnp.zeros_like(hy_k[1])

    @pl.when(z == 0)
    def _():
        hz[0] = jnp.zeros_like(hz[0])

    @pl.when(z == nz - 1)
    def _():
        hz[1] = jnp.zeros_like(hz[1])

    row = rows((cy, cz))

    def step_layer(i):
        z_low, z_high = hz[0], hz[1]

        def y_sides(values, below, above):
            plus = jnp.where(row == cy - 1, above, pltpu.roll(values, cy - 1, 0))
            minus = jnp.where(row == 0, below, pltpu.roll(values, 1, 0))
            return plus, minus

        def z_sides(values, a):
            spot = a * cx + i
            plus = jnp.where(
                lane == cz - 1, pltpu.roll(z_high, cz - 1 - spot, 1), pltpu.roll(values, cz - 1, 1)
            )
            minus = jnp.where(lane == 0, pltpu.roll(z_low, cz - spot, 1), pltpu.roll(values, 1, 1))
            return plus, minus

        center_k = k_pad[i + 1]
        k_sides = [
            (k_pad[i + 2], k_pad[i]),
            y_sides(center_k, hy_k[0, pl.ds(i, 1)], hy_k[1, pl.ds(i, 1)]),
            z_sides(center_k, 4),
        ]
        v_sides = [
            (vx_pad[i + 2], vx_pad[i]),
            y_sides(vyz[0, i], hy_v[0, pl.ds(i, 1)], hy_v[1, pl.ds(i, 1)]),
            z_sides(vyz[1, i], 3),
        ]
        faces = [(0.5 * (plus + center_k), 0.5 * (center_k + minus)) for plus, minus in k_sides]
        speeds = [(0.5 * plus, 0.5 * minus) for plus, minus in v_sides]
        marked = pick[i] > 0.5
        for f in range(3):
            center = u_pad[f, i + 1]
            u_sides = [
                (u_pad[f, i + 2], u_pad[f, i]),
                y_sides(center, hy_u[0, f, pl.ds(i, 1)], hy_u[1, f, pl.ds(i, 1)]),
                z_sides(center, f),
            ]
            terms = []
            for (k_up, k_down), (v_up, v_down), (plus, minus) in zip(faces, speeds, u_sides):
                terms.append(
                    k_up * (plus - center) - k_down * (center - minus) - (v_up * plus - v_down * minus)
                )
            fresh = center + (terms[0] + terms[1] + terms[2])
            new_vmem[f, i] = fresh
            chosen[f, i] = jnp.where(marked, fresh, 0.0).astype(jnp.bfloat16)

    def step_layers(group, carry):
        for i in range(UNROLL):
            step_layer(group * UNROLL + i)
        return carry

    lax.fori_loop(0, cx // UNROLL, step_layers, 0)
    store = pltpu.make_async_copy(new_vmem, new_hbm, store_sem)
    store.start()

    arrived(parts, mat_recv, plane - 1)
    zparts[z] = jnp.sum(parts[...], axis=0)
    to_line(zparts, zmat_send, zmat_recv)

    spots = 3 * cx * cy
    by_row = jnp.dot(
        chosen[...].reshape(spots, cz),
        (lax.div(rows(square), STRIDE) == lax.rem(lanes(square), samples)).astype(jnp.bfloat16),
        preferred_element_type=jnp.float32,
    ).reshape(spots // group, group, cz)
    own = lax.div(lanes((1, group, cz)), samples) == rows((1, group, cz))
    fresh_rows = jnp.sum(jnp.where(own, by_row, 0.0), axis=1)
    column[...] = jnp.zeros_like(column)
    for i in range(spots // group):
        column[0:1, i * cz:(i + 1) * cz] = fresh_rows[i:i + 1]
    line = lax.dot_general(
        column[...].astype(jnp.bfloat16), snaps[...], (((1,), (1,)), ((), ())),
        preferred_element_type=jnp.float32,
    )
    own_square = jnp.sum(jnp.sum(fresh_rows * fresh_rows, axis=0, keepdims=True), axis=1, keepdims=True)
    last = lanes((1, SNAPS)) == SNAPS - 1
    column[:, 0:SNAPS - 1] = line
    col_parts[me] = jnp.where(last, own_square, column[0:1, 0:SNAPS])

    to_plane(lambda peer: col_parts.at[me], col_parts.at[me], col_send, col_recv)

    arrived(zparts, zmat_recv, nz - 1)
    scale = 1.0 / (s_hbm.shape[1] * plane * nz)
    full[me] = jnp.sum(zparts[...], axis=0) * scale
    to_plane(lambda peer: full.at[me], full.at[me], all_send, all_recv)

    arrived(col_parts, col_recv, plane - 1)
    col_zparts[z] = jnp.sum(col_parts[...], axis=0)
    to_line(col_zparts, zcol_send, zcol_recv)

    arrived(full, all_recv, plane - 1)
    for i in range(plane):
        gram_ref[i * per:(i + 1) * per] = full[i]
    arrived(col_zparts, zcol_recv, nz - 1)
    gram_ref[SNAPS - 1:SNAPS] = jnp.sum(col_zparts[...], axis=0) * scale

    store.wait()
    for halo in halos:
        halo.wait_send()
    arrived(pieces, mat_send, plane - 1)
    arrived(zparts, zmat_send, nz - 1)
    arrived(full, all_send, plane - 1)
    arrived(col_parts, col_send, plane - 1)
    arrived(col_zparts, zcol_send, nz - 1)


def factor_kernel(gram_ref, new_in, r_ref, new_out, held, sem_in, sem_out):
    size, edge = gram_ref.shape[0], 8
    blocks = size // edge
    tile = (edge, size)
    fetch = pltpu.make_async_copy(new_in, held, sem_in)
    keep = pltpu.make_async_copy(held, new_out, sem_out)
    fetch.start()

    def across(values, at):
        return jnp.broadcast_to(values[:, at:at + 1], tile)

    def down(values, at):
        return jnp.broadcast_to(values[at:at + 1], tile)

    last_lane = lanes(tile) == size - 1
    turned = jnp.transpose(gram_ref[size - edge:size])
    raw = [gram_ref[t * edge:(t + 1) * edge] for t in range(blocks)]
    work = [
        jnp.where(last_lane, turned[t * edge:(t + 1) * edge, edge - 1:edge], raw[t])
        for t in range(blocks)
    ]
    sub = rows(tile)

    for b in range(blocks):
        if b == blocks // 2:
            fetch.wait()
            keep.start()
        base = b * edge
        ahead = b + 1 < blocks
        source = raw if b == 0 else work
        column = [across(source[b], base + i) for i in range(edge)]
        line = [down(work[b], i) for i in range(edge)]
        if ahead:
            side = [across(source[b + 1], base + i) for i in range(edge)]
            following = work[b + 1]
        panel = ratios = pivots = None
        for i in range(edge):
            pivot = down(column[i], i)
            inverse = pl.reciprocal(pivot, approx=False)
            ratio = [down(column[j], i) * inverse if j > i else None for j in range(edge)]
            ratio_line = line[i] * inverse
            for j in range(i + 1, edge):
                column[j] = column[j] - ratio[j] * column[i]
            for j in range(i + 1, edge):
                line[j] = line[j] - ratio[j] * line[i]
            if ahead:
                following = following - side[i] * ratio_line
                for j in range(i + 1, edge):
                    side[j] = side[j] - ratio[j] * side[i]
            panel = line[i] if i == 0 else jnp.where(sub == i, line[i], panel)
            ratios = ratio_line if i == 0 else jnp.where(sub == i, ratio_line, ratios)
            pivots = pivot if i == 0 else jnp.where(sub == i, pivot, pivots)
        r_ref[base:base + edge] = jnp.where(
            lanes(tile) >= sub + base, panel * lax.rsqrt(pivots), 0.0
        )
        if ahead:
            work[b + 1] = following
        if b + 2 < blocks:
            flipped = jnp.transpose(ratios)
            near = (b + 2) * edge
            terms = [across(flipped[near:near + edge], i) * line[i] for i in range(edge)]
            while len(terms) > 1:
                terms = [p + q for p, q in zip(terms[::2], terms[1::2])]
            work[b + 2] = work[b + 2] - terms[0]
        if b + 3 < blocks:
            far = (b + 3) * edge
            update = jnp.dot(
                flipped[far:], panel, precision=lax.Precision.HIGHEST,
                preferred_element_type=jnp.float32,
            )
            for t in range(b + 3, blocks):
                work[t] = work[t] - update[t * edge - far:(t + 1) * edge - far]
    keep.wait()


def per_device(sizes, fields, diffusivity, velocity, stored_snapshots, sample_index):
    nx, ny, nz = sizes
    plane = nx * ny
    _, cx, cy, cz = fields.shape
    per = SNAPS // plane
    f32, dma = jnp.float32, pltpu.SemaphoreType.DMA
    anywhere = pl.BlockSpec(memory_space=pl.ANY)
    vmem = pl.BlockSpec(memory_space=pltpu.VMEM)
    index = sample_index.reshape(-1, cz)
    new_fields, gram = pl.pallas_call(
        functools.partial(step_kernel, sizes),
        out_shape=(
            jax.ShapeDtypeStruct(fields.shape, f32),
            jax.ShapeDtypeStruct((SNAPS, SNAPS), f32),
        ),
        in_specs=[anywhere] * 5,
        out_specs=(anywhere, vmem),
        scratch_shapes=[
            pltpu.VMEM(index.shape, jnp.int32),
            pltpu.VMEM((3, cx + 2, cy, cz), f32),
            pltpu.VMEM((cx + 2, cy, cz), f32),
            pltpu.VMEM((cx + 2, cy, cz), f32),
            pltpu.VMEM((2, cx, cy, cz), f32),
            pltpu.VMEM(stored_snapshots.shape, jnp.bfloat16),
            pltpu.VMEM((3, cx, cy, cz), f32),
            pltpu.VMEM((2, 3, cx, cz), f32),
            pltpu.VMEM((2, cx, cz), f32),
            pltpu.VMEM((2, cx, cz), f32),
            pltpu.VMEM((2, cy, cz), f32),
            pltpu.VMEM((2, cy, cz), f32),
            pltpu.VMEM((cx, cy, cz), f32),
            pltpu.VMEM((3, cx, cy, cz), jnp.bfloat16),
            pltpu.VMEM((8, stored_snapshots.shape[1]), f32),
            pltpu.VMEM((plane, per, SNAPS), f32),
            pltpu.VMEM((plane, per, SNAPS), f32),
            pltpu.VMEM((nz, per, SNAPS), f32),
            pltpu.VMEM((plane, per, SNAPS), f32),
            pltpu.VMEM((plane, 1, SNAPS), f32),
            pltpu.VMEM((nz, 1, SNAPS), f32),
            dma((6,)),
            dma,
            dma((6, 3)),
            dma((6, 3)),
        ] + [dma] * 10,
        compiler_params=pltpu.CompilerParams(collective_id=0, has_side_effects=True),
        name="step",
    )(fields, diffusivity, velocity, stored_snapshots, index)
    snapshot_r, new_fields = pl.pallas_call(
        factor_kernel,
        out_shape=(
            jax.ShapeDtypeStruct((SNAPS, SNAPS), f32),
            jax.ShapeDtypeStruct(fields.shape, f32),
        ),
        in_specs=[vmem, anywhere],
        out_specs=(vmem, anywhere),
        scratch_shapes=[pltpu.VMEM(fields.shape, f32), dma, dma],
        name="factor",
    )(gram, new_fields)
    return (new_fields, snapshot_r)


def solution(mesh):
    sizes = tuple(mesh.shape[axis] for axis in ("gx", "gy", "gz"))
    placed = (
        P(None, "gx", "gy", "gz"),
        P("gx", "gy", "gz"),
        P(None, "gx", "gy", "gz"),
        P(None, ("gx", "gy", "gz")),
        P(("gx", "gy", "gz")),
    )
    return jax.shard_map(
        functools.partial(per_device, sizes),
        mesh=mesh,
        in_specs=placed,
        out_specs=(P(None, "gx", "gy", "gz"), P()),
        check_vma=False,
    )
```
